32 devices in a mesh: ka: 8 (over z, y), row: 4 (over x, core).
Axes of the slice: x: 2, y: 2, z: 4, core: 2. Of those that a mesh axis runs over, the one named last changes fastest.
Arguments:
- packet: float32 [16, 384, 128, 128], P('ka', None, 'row'), may hold values from -6 to 6
- previous: float32 [16, 384, 128, 128], P('ka', None, 'row'), may hold values from -6 to 6
- basis_sizes: int32 [16], P('ka'), may hold values from 96 to 384, as said below
- centrifugal: float32 [16, 384], P('ka'), may hold values from 0.1 to 2
- coriolis: float32 [16, 384], replicated, may hold values from -3 to 3
- inertia: float32 [128, 128], replicated, may hold values from 0.25 to 4
- damping: float32 [128], P('row'), may hold values from 0.6 to 1
- radial_kin: float32 [128, 128], replicated, may hold values from -0.5 to 0.5
- stretch_kin: float32 [128, 128], replicated, may hold values from -0.5 to 0.5
- legendre: float32 [16, 512, 384], P('ka'), may hold values from -0.3125 to 0.3125
- potential: float32 [512, 128, 128], P(None, 'row'), may hold values from -1 to 1
Outputs:
- advanced: float32 [16, 384, 128, 128], P('ka', None, 'row')
The draws below stay inside these ranges and needn't reach their ends.
Inputs may be any that keep to these rules, and one draw needn't show every extreme that they name: `basis_sizes`: one helicity block has exactly 384 live basis functions and another exactly 96.
All inputs are finite; a program needn't handle non-finite values.
Results may differ from the reference program's by a relative error of at most 0.0003.
Values sent between devices are 32-bit elements; how exact they have to be, the bound alone decides.
A program may use at most 192 MiB of HBM per device.

```python
import math
import jax
import jax.numpy as jnp
from jax import lax

JMAX = 384
NANG = 512
NR = 128
NRR = 128
NK = 16


def draw_basis_sizes(key, part):
    block_sizes = jax.random.randint(jax.random.fold_in(key, 11), (NK,), JMAX // 4, JMAX + 1)
    shuffled = jax.random.permutation(jax.random.fold_in(key, 17), NK)
    block_sizes = block_sizes.at[shuffled[0]].set(JMAX)
    block_sizes = block_sizes.at[shuffled[1]].set(JMAX // 4)
    return block_sizes.astype(jnp.int32)


def level_of(rng, dims, split, low, largest):
    loudness = 1.0
    for dim, shards_of in split:
        draws = jax.random.uniform(jax.random.fold_in(jax.random.fold_in(rng, 6), dim), (shards_of,), jnp.float32, low / len(split), largest / len(split))
        loudness = loudness * jnp.repeat(jnp.exp(draws), dims[dim] // shards_of).reshape((-1,) + (1,) * (len(dims) - 1 - dim))
    return loudness


def bell_draw(rng, dims, spread, bound, cuts=(), held_as=jnp.bfloat16):
    values = spread * jax.random.normal(rng, dims, jnp.float32)
    if cuts:
        values = values * level_of(rng, dims, cuts, -0.22, 0.18)
    return jnp.clip(values, -bound, bound).astype(held_as)


def setup_inputs(seed: int = 0) -> dict:
    streams_of = jax.random.split(jax.random.key(seed), 12)
    packet = bell_draw(streams_of[0], (NK, JMAX, NR, NRR), 1.0, 6.0, ((0, 8), (2, 4)), jnp.float32)
    previous = bell_draw(streams_of[1], (NK, JMAX, NR, NRR), 1.0, 6.0, ((0, 8), (2, 4)), jnp.float32)
    basis_sizes = draw_basis_sizes(jax.random.fold_in(streams_of[11], 71), 0)
    centrifugal = jnp.clip(jnp.exp(math.log(2.0) - 2.9957323 * jax.random.uniform(streams_of[3], (NK, JMAX), jnp.float32) ** level_of(streams_of[3], (NK, JMAX), ((0, 8),), -0.2, 0.2)), 0.1, 2.0)
    coriolis = bell_draw(streams_of[4], (NK, JMAX), 0.5, 3.0, (), jnp.float32)
    inertia = jnp.clip(jnp.exp(jax.random.uniform(streams_of[5], (NR, NRR), jnp.float32, math.log(0.25), math.log(4.0))), 0.25, 4.0)
    damping = jnp.clip(0.6 + 0.39999998 * jax.random.uniform(streams_of[6], (NR,), jnp.float32) ** level_of(streams_of[6], (NR,), ((0, 4),), -0.2, 0.2), 0.6, 1.0)
    radial_kin = bell_draw(streams_of[7], (NR, NR), NR ** -0.5, 0.5, (), jnp.float32)
    stretch_kin = bell_draw(streams_of[8], (NRR, NRR), NRR ** -0.5, 0.5, (), jnp.float32)
    legendre = bell_draw(streams_of[9], (NK, NANG, JMAX), JMAX ** -0.5, 0.3125, ((0, 8),), jnp.float32)
    potential = jnp.clip(jax.random.uniform(streams_of[10], (NANG, NR, NRR), jnp.float32, -1.0, 1.0) * level_of(streams_of[10], (NANG, NR, NRR), ((1, 4),), -0.4, 0.0), -1.0, 1.0)
    return {"packet": packet, "previous": previous, "basis_sizes": basis_sizes, "centrifugal": centrifugal, "coriolis": coriolis, "inertia": inertia, "damping": damping, "radial_kin": radial_kin, "stretch_kin": stretch_kin, "legendre": legendre, "potential": potential}


def reference(packet, previous, basis_sizes, centrifugal, coriolis, inertia, damping, radial_kin, stretch_kin, legendre, potential):
    precise = lax.Precision.HIGHEST
    basis_index = jnp.arange(JMAX, dtype=jnp.int32)
    live_mask = (basis_index[None, :] < basis_sizes[:, None]).astype(jnp.float32)

    def fetch(position):
        clipped = jnp.clip(position, 0, NK - 1).astype(jnp.int32)
        in_range = ((position >= 0) & (position < NK)).astype(jnp.float32)
        block = lax.dynamic_index_in_dim(packet, clipped, 0, keepdims=False)
        row_mask = lax.dynamic_index_in_dim(live_mask, clipped, 0, keepdims=False)
        return block * row_mask[:, None, None] * in_range

    def one_block(block_id):
        masked = fetch(block_id)
        upper_block = fetch(block_id + 1)
        lower_block = fetch(block_id - 1)
        coupling_here = lax.dynamic_index_in_dim(coriolis, block_id, 0, keepdims=False)
        coupling_before = lax.dynamic_index_in_dim(coriolis, jnp.maximum(block_id - 1, 0).astype(jnp.int32), 0, keepdims=False)
        radial_term = jnp.einsum('rs,jsx->jrx', radial_kin, masked, precision=precise) + jnp.einsum('jrz,xz->jrx', masked, stretch_kin, precision=precise)
        rotation_term = lax.dynamic_index_in_dim(centrifugal, block_id, 0, keepdims=False)[:, None, None] * inertia[None] * masked
        angular = lax.dynamic_index_in_dim(legendre, block_id, 0, keepdims=False)
        on_grid = jnp.einsum('gj,jy->gy', angular, masked.reshape(JMAX, NR * NRR), precision=precise) * potential.reshape(NANG, NR * NRR)
        potential_term = jnp.einsum('gj,gy->jy', angular, on_grid, precision=precise).reshape(JMAX, NR, NRR)
        coupling_term = inertia[None] * (coupling_here[:, None, None] * upper_block + coupling_before[:, None, None] * lower_block)
        hamilton = radial_term + rotation_term + potential_term + coupling_term
        earlier = lax.dynamic_index_in_dim(previous, block_id, 0, keepdims=False)
        row_mask = lax.dynamic_index_in_dim(live_mask, block_id, 0, keepdims=False)
        factor = damping[None, :, None]
        return row_mask[:, None, None] * factor * (2.0 * hamilton - factor * earlier)

    return lax.map(one_block, jnp.arange(NK, dtype=jnp.int32))
```

```python
import functools

import jax
import jax.numpy as jnp
from jax import lax
from jax.experimental import pallas as pl
from jax.experimental.pallas import tpu as pltpu
from jax.sharding import PartitionSpec as P


HALVES = 2


def from_behind(x, axis, by):
    peers = lax.axis_size(axis)
    pairs = [(i, i + by) for i in range(peers) if 0 <= i + by < peers]
    return lax.ppermute(x, axis, pairs)


def rotate(x, by):
    peers = lax.axis_size("row")
    return lax.ppermute(x, "row", [(i, (i + by) % peers) for i in range(peers)])


def swap_cores(x):
    peers = lax.axis_size("row")
    return lax.ppermute(x, "row", [(i, i ^ 1) for i in range(peers)])


def split_bf16(x):
    high = x.astype(jnp.bfloat16)
    return high, (x - high.astype(jnp.float32)).astype(jnp.bfloat16)


def finish_kernel(block, base, sources, remotes, *refs):
    kin_ref, live_ref = refs[0], refs[1]
    factor_ref, turn_ref = refs[2], refs[3]
    source_refs = refs[4 : 4 + sources]
    remote_refs = refs[4 + sources : 4 + sources + 2 * remotes]
    acc_ref, out_ref = refs[-2], refs[-1]
    tile = out_ref.shape[1]
    rows = out_ref.shape[2]
    width = out_ref.shape[3]
    first = base + pl.program_id(0) * tile
    stacked = jnp.concatenate(
        [jnp.concatenate([ref[0, j] for j in range(tile)], axis=1) for ref in source_refs], axis=0
    )
    high, low = split_bf16(stacked)
    both = jnp.dot(kin_ref[...], high, preferred_element_type=jnp.float32)
    rest = jnp.dot(kin_ref[:rows, :], low, preferred_element_type=jnp.float32)
    radial = both[:rows] + both[rows:] + rest
    factor = factor_ref[...]
    turn = turn_ref[...]
    for j in range(tile):
        term = factor * radial[:, j * width : (j + 1) * width]
        for n in range(remotes):
            values, weights = remote_refs[2 * n], remote_refs[2 * n + 1]
            term = term + turn * (weights[block, first + j] * values[0, j])
        out_ref[0, j] = acc_ref[0, j] + live_ref[block, first + j] * term


def finish(acc, block, base, count, kin, live, factor, turn, sources, remotes):
    _, basis_len, rows, width = acc.shape
    tile = next(t for t in (32, 24, 16, 8, 4, 2, 1) if count % t == 0 and base % t == 0)
    whole = lambda i: (block, base // tile + i, 0, 0)
    part = lambda i: (0, i, 0, 0)
    shape = (1, tile, rows, width)
    vmem = lambda x: pl.BlockSpec(x.shape, lambda i: (0,) * x.ndim)
    smem = pl.BlockSpec(memory_space=pltpu.SMEM)
    operands = [kin, live, factor, turn]
    specs = [vmem(kin), smem, vmem(factor), vmem(turn)]
    for x in sources:
        operands.append(x)
        specs.append(pl.BlockSpec(shape, whole if x.shape[1] == basis_len else part))
    for x, weights in remotes:
        operands += [x, weights]
        specs += [pl.BlockSpec(shape, part), smem]
    operands.append(acc)
    specs.append(pl.BlockSpec(shape, whole))
    size = count * rows * width
    return pl.pallas_call(
        functools.partial(finish_kernel, block, base, len(sources), len(remotes)),
        out_shape=jax.ShapeDtypeStruct(acc.shape, acc.dtype),
        grid=(count // tile,),
        in_specs=specs,
        out_specs=pl.BlockSpec(shape, whole),
        input_output_aliases={len(operands) - 1: 0},
        cost_estimate=pl.CostEstimate(
            flops=6 * size * rows * len(sources),
            bytes_accessed=4 * size * (2 + len(sources) + len(remotes)),
            transcendentals=0,
        ),
        compiler_params=pltpu.CompilerParams(vmem_limit_bytes=40 << 20),
        name="finish",
    )(*operands)


def shards(
    packet,
    previous,
    basis_sizes,
    centrifugal,
    coriolis,
    inertia,
    damping,
    radial_kin,
    stretch_kin,
    legendre,
    potential,
):
    precise = lax.Precision.HIGH
    blocks, basis_len, rows, width = packet.shape
    peers = lax.axis_size("row")
    ka_index = lax.axis_index("ka")
    row_index = lax.axis_index("row")
    basis_index = lax.broadcasted_iota(jnp.int32, (blocks, basis_len), 1)
    live = (basis_index < basis_sizes[:, None]).astype(jnp.float32)
    coupling = lax.dynamic_slice_in_dim(coriolis, ka_index * blocks, blocks, 0)
    ones = jnp.ones_like(live)

    count = basis_len // HALVES
    order = [(b, h * count) for h in range(HALVES) for b in range(blocks)]
    piece = lambda x, b, at: x[b : b + 1, at : at + count]
    scaled = lambda x, w, b, at: piece(x, b, at) * piece(w, b, at)[:, :, None, None]

    crossed, uppers, lowers = {}, {}, {}
    for b, at in order:
        mine = scaled(packet, live, b, at)
        crossed[b, at] = [rotate(mine, 2 * d) for d in range(1, peers // 2)]
        if b == 0:
            uppers[at] = from_behind(mine, "ka", -1)
        if b == blocks - 1:
            weighted = scaled(packet, live * coupling, b, at)
            lowers[at] = from_behind(weighted, "ka", 1)
    masked = packet * live[:, :, None, None]
    partner = swap_cores(masked)

    inertia_local = lax.dynamic_slice_in_dim(inertia, row_index * rows, rows, 0)
    flattened = masked.reshape(blocks, basis_len, rows * width)
    on_grid = jnp.einsum("kgj,kjy->kgy", legendre, flattened, precision=precise)
    on_grid = (
        on_grid
        * potential.reshape(potential.shape[0], rows * width)[None]
    )
    potential_term = jnp.einsum("kgj,kgy->kjy", legendre, on_grid, precision=precise).reshape(
        masked.shape
    )
    along_bonds = jnp.einsum("kjrz,xz->kjrx", masked, stretch_kin, precision=precise)
    inside = []
    for b in range(blocks):
        term = centrifugal[b][:, None, None] * masked[b]
        if b + 1 < blocks:
            term = term + coupling[b][:, None, None] * masked[b + 1]
        if b > 0:
            term = term + coupling[b - 1][:, None, None] * masked[b - 1]
        inside.append(term)
    inside = inertia_local[None, None] * jnp.stack(inside)
    hamilton = potential_term + along_bonds + inside
    factor = damping[None, None, :, None]
    acc = live[:, :, None, None] * factor * (2.0 * hamilton - factor * previous)

    kin = lax.dynamic_slice_in_dim(radial_kin, row_index * rows, rows, 0)
    origins = [row_index, row_index ^ 1]
    for d in range(1, peers // 2):
        origin = (row_index - 2 * d) % peers
        origins += [origin, origin ^ 1]
    kin = jnp.concatenate(
        [lax.dynamic_slice_in_dim(kin, origin * rows, rows, 1) for origin in origins], 1
    )
    rounded = lax.reduce_precision(kin, 8, 7)
    kin = jnp.concatenate([rounded, kin - rounded], 0).astype(jnp.bfloat16)
    doubled = jnp.broadcast_to(2.0 * damping[:, None], (rows, width))
    turn = doubled * inertia_local
    for b, at in order:
        arrived, acc = lax.optimization_barrier((crossed[b, at], acc))
        sources = [masked, partner]
        for x in arrived:
            sources += [x, swap_cores(x)]
        remotes = []
        if b == 0:
            remotes.append((lowers[at], ones))
        if b == blocks - 1:
            remotes.append((uppers[at], coupling))
        acc = finish(acc, b, at, count, kin, live, doubled, turn, sources, remotes)
    return acc


def solution(mesh):
    in_specs = (
        P("ka", None, "row", None),
        P("ka", None, "row", None),
        P("ka"),
        P("ka", None),
        P(),
        P(),
        P("row"),
        P(),
        P(),
        P("ka", None, None),
        P(None, "row", None),
    )
    out_specs = P("ka", None, "row", None)

    return jax.shard_map(
        shards, mesh=mesh, in_specs=in_specs, out_specs=out_specs, check_vma=False
    )
```
